32 devices in a mesh: fsdp: 16 (over z, x, core), tp: 2 (over y).
Axes of the slice: x: 2, y: 2, z: 4, core: 2. Of those that a mesh axis runs over, the one named last changes fastest.
Arguments:
- activations: bfloat16 [4096, 2048], P(('fsdp', 'tp')), may hold values from -6 to 6
- cotangent: bfloat16 [4096, 2048], P(('fsdp', 'tp')), may hold values from -6 to 6
- segment_ids: int32 [16, 256], P('fsdp'), may hold values from 0 to 2, never falling along the last dimension, each value on 1 to 128 neighbouring positions
- routes: int32 [4096, 8], P('fsdp'), may hold values from 0 to 15, all different within a row; in each aligned block of 256 rows (0 to 255, 256 to 511, ...) at most 128 rows name the same one
- w_query: bfloat16 [2048, 4096], P('fsdp', 'tp'), may hold values from -0.125 to 0.125
- key_matrix: bfloat16 [2048, 512], P('fsdp', 'tp'), may hold values from -0.125 to 0.125
- value_matrix: bfloat16 [2048, 512], P('fsdp', 'tp'), may hold values from -0.125 to 0.125
- w_out: bfloat16 [4096, 2048], P('tp', 'fsdp'), may hold values from -0.375 to 0.375
- w_router: bfloat16 [2048, 16], P('fsdp'), may hold values from -0.125 to 0.125
- gain_attn: bfloat16 [2048], P('fsdp'), may hold values from 0.25 to 1.75
- gain_moe: bfloat16 [2048], P('fsdp'), may hold values from 0.25 to 1.75
- gain_query: bfloat16 [128], P('fsdp'), may hold values from 0.25 to 1.75
- gain_key: bfloat16 [128], P('fsdp'), may hold values from 0.25 to 1.75
- w_gate: bfloat16 [16, 2048, 768], P('fsdp', None, 'tp'), may hold values from -0.125 to 0.125
- w_up: bfloat16 [16, 2048, 768], P('fsdp', None, 'tp'), may hold values from -0.125 to 0.125
- w_down: bfloat16 [16, 768, 2048], P('fsdp', 'tp'), may hold values from -0.625 to 0.625
Outputs:
- block_out: bfloat16 [4096, 2048], P(('fsdp', 'tp'))
- grad_input: bfloat16 [4096, 2048], P(('fsdp', 'tp'))
- grad_query: float32 [2048, 4096], P('fsdp', 'tp')
- grad_key: float32 [2048, 512], P('fsdp', 'tp')
- grad_value: float32 [2048, 512], P('fsdp', 'tp')
- grad_out: float32 [4096, 2048], P('tp', 'fsdp')
- grad_router: float32 [2048, 16], P(('fsdp', 'tp'))
- grad_gain_attn: float32 [2048], P(('fsdp', 'tp'))
- grad_gain_moe: float32 [2048], P(('fsdp', 'tp'))
- grad_gain_query: float32 [128], P(('fsdp', 'tp'))
- grad_gain_key: float32 [128], P(('fsdp', 'tp'))
- grad_gate: float32 [16, 2048, 768], P('fsdp', None, 'tp')
- grad_up: float32 [16, 2048, 768], P('fsdp', None, 'tp')
- grad_down: float32 [16, 768, 2048], P('fsdp', 'tp')
The draws below stay inside these ranges and needn't reach their ends.
Inputs may be any that keep to these rules, and one draw needn't show every extreme that they name: `routes`: each token names 8 different experts. Within the tokens of one pack (256 aligned rows) every expert is named by exactly 128 tokens. `segment_ids`: within a pack the values never fall; each document spans at most 128 tokens, and some document spans exactly that many.
All inputs are finite; a program needn't handle non-finite values.
Results may differ from the reference program's by a relative error of at most 0.025.
Values may be sent and summed in bfloat16 or wider, within the bound.
No kernel may reach another device: no remote copies, remote signals or barrier semaphores. Data moves between devices by JAX's collectives and lax.ppermute only.
A program may use at most 256 MiB of HBM per device.

```python
import math
import jax
import jax.numpy as jnp
import numpy as np
from jax import lax

MODEL_DIM = 2048
QUERY_HEADS = 32
KEY_VALUE_HEADS = 4
HEAD_DIM = 128
FF = 768
TOPK = 8
DOCS = 3
PACK = 256
PACKS = 16
TOKENS = 4096
EXPERTS = 16
CAP = 128
N_TP = 2


def levels(own_key, dims, shards, least, top_value):
    factor_of, own = 1.0, jax.random.fold_in(own_key, 6)
    for dim, parts in shards:
        draws = jnp.exp(jax.random.uniform(jax.random.fold_in(own, dim), (parts,), jnp.float32, least / len(shards), top_value / len(shards)))
        factor_of = factor_of * jnp.repeat(draws, dims[dim] // parts).reshape([-1 if axis == dim else 1 for axis in range(len(dims))])
    return factor_of


def split_up(amount, total, limit, skew):
    portions = [(1 << 20) // math.isqrt(grade ** skew) + 1 for grade in range(2, amount + 1)]
    surplus, holding = total - limit - (amount - 1), [1] * (amount - 1)
    while surplus > 0:
        candidates = [i for i in range(amount - 1) if holding[i] < limit]
        whole, left = sum([portions[i] for i in candidates]), surplus
        for i in candidates:
            extra = min(limit - holding[i], max(1, left * portions[i] // whole), surplus)
            holding[i] = holding[i] + extra
            surplus = surplus - extra
    return np.array([limit] + holding)


def uneven(stream_key, amount, total, limit, skew):
    if amount == 2:
        one = jax.random.randint(stream_key, (), max(1, total - limit), min(limit, total - 1) + 1)
        return jnp.stack([one, total - one])
    lengths = jnp.asarray(split_up(amount, total, limit, skew), jnp.int32)
    pairs = (amount - 1) // 2
    source_of, receiver = lengths[1:1 + 2 * pairs:2], lengths[2:2 + 2 * pairs:2]
    margin = jnp.minimum(source_of - 1, limit - receiver)
    passed = jax.random.randint(jax.random.fold_in(stream_key, 1), (pairs,), 0, 1 << 20) % (margin + 1)
    lengths = lengths.at[1:1 + 2 * pairs:2].set(source_of - passed).at[2:2 + 2 * pairs:2].set(receiver + passed)
    return lengths[jax.random.permutation(jax.random.fold_in(stream_key, 2), amount)]


def routed_block(key, own, number, rows, amount, top, limit, lean):
    sequence = jax.random.permutation(key, amount)
    packed, usual = shares(amount, rows * top, limit, lean, True), shares(amount, rows * top, limit, lean, False)
    places = jnp.arange(amount)

    def named(sizes, rotation):
        used = int((sizes > 0).sum())
        fixed = max(1, used // 4)
        passed = fixed + (places - fixed + rotation * (used - fixed)) % max(1, amount - fixed)
        return jnp.zeros((amount,), jnp.int32).at[sequence[jnp.where(places < fixed, places, passed)]].set(jnp.asarray(sizes, jnp.int32))

    sizes = jnp.where(number % 4 == 0, named(packed, number // 4), named(usual, number - number // 4 - 1))
    mixed = jax.random.permutation(jax.random.fold_in(own, 3), amount)
    donor, taker = mixed[0:amount // 2 * 2:2], mixed[1:amount // 2 * 2:2]
    slack = jnp.minimum(sizes[donor] - 1, limit - sizes[taker]) // 2
    slack = jnp.where((donor == sequence[0]) | (taker == sequence[0]) | (sizes[taker] == 0), 0, jnp.maximum(slack, 0))
    passed = jax.random.randint(jax.random.fold_in(own, 4), (amount // 2,), 0, 1 << 20) % (slack + 1)
    sizes = sizes.at[donor].add(-passed).at[taker].add(passed)
    items = jnp.searchsorted(jnp.cumsum(sizes), jnp.arange(rows * top), side="right").astype(jnp.int32)
    listing = items.reshape(top, rows).T
    listing = listing[jax.random.permutation(jax.random.fold_in(own, 1), rows)]
    rotation = jax.random.randint(jax.random.fold_in(own, 2), (rows, 1), 0, top)
    return jnp.take_along_axis(listing, (jnp.arange(top)[None, :] + rotation) % top, axis=1)


def shares(count, total, limit, skew, full):
    weights = [(1 << 20) // math.isqrt(grade ** skew) + 1 for grade in range(1, count + 1)]
    largest = limit if full else min(limit, max(-(-total // count), total * weights[0] // sum(weights)))
    least = 1 if total - largest >= count - 1 else 0
    given, rest = [largest] + [least] * (count - 1), total - largest - least * (count - 1)
    while rest > 0:
        free = [i for i in range(1, count) if given[i] < largest] or [i for i in range(1, count) if given[i] < limit]
        pool, budget = sum([weights[i] for i in free]), rest
        for i in free:
            more = min(limit - given[i], max(1, budget * weights[i] // pool), rest)
            given[i] = given[i] + more
            rest = rest - more
    return np.array(given)


def gaussian(own_key, dims, spread, reach, pieces=(), kind=jnp.bfloat16):
    level = levels(own_key, dims, pieces, -0.22, 0.18) if pieces else 1.0
    entries = jax.random.normal(own_key, dims, jnp.float32) * spread * level
    return jnp.minimum(jnp.maximum(entries, -reach), reach).astype(kind)


def setup_inputs(seed: int = 0) -> dict:
    key_of = jax.random.split(jax.random.key(seed), 17)
    activations = gaussian(key_of[0], (TOKENS, MODEL_DIM), 1.0, 6.0, ((0, 32),))
    cotangent = gaussian(key_of[1], (TOKENS, MODEL_DIM), 1.0, 6.0, ((0, 32),))
    segment_ids = jax.vmap(lambda own: jnp.searchsorted(jnp.cumsum(uneven(own, DOCS, PACK, PACK // 2, 1)), jnp.arange(PACK), side="right"))(jax.random.split(key_of[2], PACKS)).reshape((PACKS, PACK)).astype(jnp.int32)
    routes_keys = jax.random.split(jax.random.fold_in(key_of[3], 1), TOKENS // PACK)
    routes_turns = jax.random.permutation(jax.random.fold_in(key_of[3], 3), TOKENS // PACK)
    routes = jax.vmap(lambda own, number: routed_block(jax.random.fold_in(key_of[3], 2), own, number, PACK, EXPERTS, TOPK, CAP, 0))(routes_keys, routes_turns).reshape((TOKENS, TOPK))
    w_query = gaussian(key_of[4], (MODEL_DIM, QUERY_HEADS * HEAD_DIM), MODEL_DIM ** -0.5, 0.125, ((0, 16), (1, 2)))
    key_matrix = gaussian(key_of[5], (MODEL_DIM, KEY_VALUE_HEADS * HEAD_DIM), MODEL_DIM ** -0.5, 0.125, ((0, 16), (1, 2)))
    value_matrix = gaussian(key_of[6], (MODEL_DIM, KEY_VALUE_HEADS * HEAD_DIM), MODEL_DIM ** -0.5, 0.125, ((0, 16), (1, 2)))
    w_out = gaussian(key_of[7], (QUERY_HEADS * HEAD_DIM, MODEL_DIM), (QUERY_HEADS * HEAD_DIM // 16) ** -0.5, 0.375, ((0, 2), (1, 16)))
    w_router = gaussian(key_of[8], (MODEL_DIM, EXPERTS), MODEL_DIM ** -0.5, 0.125, ((0, 16),))
    gain_attn = jnp.clip(1.0 + 0.15 * jax.random.normal(key_of[9], (MODEL_DIM,), jnp.float32), 0.25, 1.75).astype(jnp.bfloat16)
    gain_moe = jnp.clip(1.0 + 0.15 * jax.random.normal(key_of[10], (MODEL_DIM,), jnp.float32), 0.25, 1.75).astype(jnp.bfloat16)
    gain_query = jnp.clip(1.0 + 0.15 * jax.random.normal(key_of[11], (HEAD_DIM,), jnp.float32), 0.25, 1.75).astype(jnp.bfloat16)
    gain_key = jnp.clip(1.0 + 0.15 * jax.random.normal(key_of[12], (HEAD_DIM,), jnp.float32), 0.25, 1.75).astype(jnp.bfloat16)
    w_gate = gaussian(key_of[13], (EXPERTS, MODEL_DIM, FF), MODEL_DIM ** -0.5, 0.125, ((0, 16), (2, 2)))
    w_up = gaussian(key_of[14], (EXPERTS, MODEL_DIM, FF), MODEL_DIM ** -0.5, 0.125, ((0, 16), (2, 2)))
    w_down = gaussian(key_of[15], (EXPERTS, FF, MODEL_DIM), (FF // 8) ** -0.5, 0.625, ((0, 16), (1, 2)))
    return {"activations": activations, "cotangent": cotangent, "segment_ids": segment_ids, "routes": routes, "w_query": w_query, "key_matrix": key_matrix, "value_matrix": value_matrix, "w_out": w_out, "w_router": w_router, "gain_attn": gain_attn, "gain_moe": gain_moe, "gain_query": gain_query, "gain_key": gain_key, "w_gate": w_gate, "w_up": w_up, "w_down": w_down}


@jax.custom_vjp
def low(v):
    return lax.optimization_barrier(v.astype(jnp.bfloat16)).astype(jnp.float32)

@jax.custom_vjp
def low_back(v):
    return v

def low_keep(v):
    return (low(v), None)

def low_pass(kept, grad):
    return (grad,)

def back_keep(v):
    return (v, None)

def back_low(kept, grad):
    return (low(grad),)
low.defvjp(low_keep, low_pass)
low_back.defvjp(back_keep, back_low)
EPS = 1e-06
ROPE_BASE = 1000000.0
HIGH = lax.Precision.HIGHEST

def matrix_product(left, right):
    return jnp.dot(left, right, precision=HIGH)

def rms_scale(value_rows, gain):
    return value_rows * lax.rsqrt(lax.optimization_barrier(jnp.mean(value_rows * value_rows, axis=-1, keepdims=True)) + EPS) * gain

def half_turn(value_rows):
    middle = value_rows.shape[-1] // 2
    return jnp.concatenate([-value_rows[..., middle:], value_rows[..., :middle]], axis=-1)

def rope_tables(segment_row):
    tally_count = segment_row.shape[0]
    index = jnp.arange(tally_count, dtype=jnp.int32)
    first_flag = jnp.concatenate([jnp.ones((1,), dtype=bool), segment_row[1:] != segment_row[:-1]])
    start = lax.cummax(jnp.where(first_flag, index, 0), axis=0)
    position = (index - start).astype(jnp.float32)
    freqs = ROPE_BASE ** (-(2.0 * jnp.arange(HEAD_DIM // 2, dtype=jnp.float32)) / HEAD_DIM)
    angle = position[:, None] * freqs[None, :]
    angle = jnp.concatenate([angle, angle], axis=-1)
    return (jnp.cos(angle), jnp.sin(angle))

def slot_index(route_rows, experts_all, capacity):
    chosen = (route_rows[:, :, None] == jnp.arange(experts_all, dtype=jnp.int32)[None, None, :]).astype(jnp.int32)
    per_token = lax.optimization_barrier(jnp.sum(chosen, axis=1))
    before = jnp.cumsum(per_token, axis=0) - per_token
    slot = lax.optimization_barrier(jnp.sum(chosen * before[:, None, :], axis=2))
    return (route_rows * capacity + slot).astype(jnp.int32)

def pack_forward(inputs, segment_row, route_rows, w_query, key_matrix, value_matrix, w_out, w_router, gain_attn, gain_moe, gain_query, gain_key, w_gate, w_up, w_down):
    tally_count = inputs.shape[0]
    cosine, sine = rope_tables(segment_row)
    attention_input = low(rms_scale(inputs, gain_attn))
    query_rows = low_back(matrix_product(attention_input, w_query)).reshape(tally_count, QUERY_HEADS, HEAD_DIM)
    key_rows = low_back(matrix_product(attention_input, key_matrix)).reshape(tally_count, KEY_VALUE_HEADS, HEAD_DIM)
    value_rows = low_back(matrix_product(attention_input, value_matrix)).reshape(tally_count, KEY_VALUE_HEADS, HEAD_DIM)
    query_rows = rms_scale(query_rows, gain_query)
    key_rows = rms_scale(key_rows, gain_key)
    query_rows = low(query_rows * cosine[:, None, :] + half_turn(query_rows) * sine[:, None, :])
    key_rows = low(key_rows * cosine[:, None, :] + half_turn(key_rows) * sine[:, None, :])
    value_rows = low(value_rows)
    head_group = QUERY_HEADS // KEY_VALUE_HEADS
    query_rows = query_rows.reshape(tally_count, KEY_VALUE_HEADS, head_group, HEAD_DIM)
    scores = low_back(jnp.einsum('iagd,jad->agij', query_rows, key_rows, precision=HIGH) * HEAD_DIM ** (-0.5))
    index = jnp.arange(tally_count, dtype=jnp.int32)
    allowed = (segment_row[:, None] == segment_row[None, :]) & (index[None, :] <= index[:, None])
    scores = jnp.where(allowed, scores, -1e+30)
    probs = low(jax.nn.softmax(scores, axis=-1))
    attended = jnp.einsum('agij,jad->iagd', probs, value_rows, precision=HIGH).reshape(tally_count, QUERY_HEADS * HEAD_DIM)
    attended = low(low_back(attended))
    middle = inputs + low_back(matrix_product(attended, w_out))
    moe_in = low(rms_scale(middle, gain_moe))
    logits = matrix_product(moe_in, w_router)
    picked = jnp.take_along_axis(logits, route_rows, axis=1)
    weights = low(jax.nn.softmax(picked, axis=-1))
    flat = slot_index(route_rows, EXPERTS, CAP).reshape(-1)
    copies = jnp.repeat(moe_in, TOPK, axis=0)
    width = FF // N_TP
    mixed = jnp.zeros((tally_count, MODEL_DIM), jnp.float32)
    for part in range(N_TP):
        entry = low_back(copies)
        buffer = jnp.zeros((EXPERTS * CAP, MODEL_DIM), jnp.float32).at[flat].add(entry).reshape(EXPERTS, CAP, MODEL_DIM)
        gate_pre = low_back(jnp.einsum('ecd,edh->ech', buffer, w_gate[:, :, part * width:(part + 1) * width], precision=HIGH))
        up_pre = low_back(jnp.einsum('ecd,edh->ech', buffer, w_up[:, :, part * width:(part + 1) * width], precision=HIGH))
        hidden = low(jax.nn.silu(gate_pre) * up_pre)
        result = jnp.einsum('ech,ehd->ecd', hidden, w_down[:, part * width:(part + 1) * width, :], precision=HIGH)
        result = low(low_back(result)).reshape(EXPERTS * CAP, MODEL_DIM)
        chosen = result[flat].reshape(tally_count, TOPK, MODEL_DIM)
        mixed = mixed + lax.optimization_barrier(jnp.sum(weights[:, :, None] * chosen, axis=1))
    return middle + low_back(mixed)

def reference(activations, cotangent, segment_ids, routes, w_query, key_matrix, value_matrix, w_out, w_router, gain_attn, gain_moe, gain_query, gain_key, w_gate, w_up, w_down):
    params = tuple((p.astype(jnp.float32) for p in (w_query, key_matrix, value_matrix, w_out, w_router, gain_attn, gain_moe, gain_query, gain_key, w_gate, w_up, w_down)))
    inputs = activations.astype(jnp.float32).reshape(PACKS, PACK, MODEL_DIM)
    grads_in = cotangent.astype(jnp.float32).reshape(PACKS, PACK, MODEL_DIM)
    route_packs = routes.reshape(PACKS, PACK, TOPK)

    def step(totals, pack):
        inputs_pack, grad_pack, segment_row, route_rows = pack

        def forward(value_rows, *weights):
            return pack_forward(value_rows, segment_row, route_rows, *weights)
        result, pullback = jax.vjp(forward, inputs_pack, *params)
        grads = pullback(grad_pack)
        totals = tuple((a + b for a, b in zip(totals, grads[1:])))
        return (totals, (result, grads[0]))
    zeros = tuple((jnp.zeros(p.shape, jnp.float32) for p in params))
    totals, (results, grad_rows) = lax.scan(step, zeros, (inputs, grads_in, segment_ids, route_packs))
    block_out = results.reshape(TOKENS, MODEL_DIM).astype(jnp.bfloat16)
    grad_input = grad_rows.reshape(TOKENS, MODEL_DIM).astype(jnp.bfloat16)
    return (block_out, grad_input, totals[0], totals[1], totals[2], totals[3], totals[4], totals[5], totals[6], totals[7], totals[8], totals[9], totals[10], totals[11])
```

```python
import jax
import jax.numpy as jnp
from jax import lax
from jax.sharding import PartitionSpec as P

EPS = 1e-06
ROPE_BASE = 1000000.0
HIGH = lax.Precision.HIGHEST
F32 = jnp.float32
BF16 = jnp.bfloat16
LANES = 128


def after(value, *deps):
    return lax.optimization_barrier((value,) + deps)[0]


def mm(eq, left, right, out=F32):
    return jnp.einsum(eq, left, right, preferred_element_type=F32).astype(out)


def norm_back(grad_after, value_rows, scale, gain):
    normed = value_rows * scale
    scaled = grad_after * gain
    grad_before = scale * (scaled - normed * jnp.mean(scaled * normed, axis=-1, keepdims=True))
    return (grad_before, grad_after * normed)


def half_turn(value_rows):
    middle = value_rows.shape[-1] // 2
    return jnp.concatenate([-value_rows[..., middle:], value_rows[..., :middle]], axis=-1)


def half_turn_back(value_rows):
    middle = value_rows.shape[-1] // 2
    return jnp.concatenate([value_rows[..., middle:], -value_rows[..., :middle]], axis=-1)


class Ring:
    def __init__(self):
        self.size = lax.axis_size("fsdp")
        self.tp = lax.axis_size("tp")
        self.place = lax.axis_index("fsdp")
        self.direct = self.size == 16

    def hop(self, value, bits):
        return lax.ppermute(value, "fsdp", [(i, i ^ bits) for i in range(self.size)])

    def swap(self, value):
        return lax.ppermute(value, "tp", [(i, i ^ 1) for i in range(self.tp)])

    def order(self, k):
        return jnp.bitwise_xor(self.place, k) if self.direct else k

    def gather(self, block):
        if not self.direct:
            return lax.all_gather(block, "fsdp", axis=0, tiled=False), block
        parts = {0: block}
        for k in (12, 8, 4):
            parts[k] = self.hop(block, k)
        for k in (0, 4, 8, 12):
            parts[k + 2] = self.hop(parts[k], 2)
        for k in range(0, 16, 2):
            parts[k + 1] = self.hop(parts[k], 1)
        whole = jnp.zeros((16,) + block.shape, block.dtype)
        for k in range(16):
            whole = lax.dynamic_update_slice_in_dim(whole, parts[k][None], self.order(k), 0)
        return whole, parts[14]

    def gather_small(self, block):
        if not self.direct:
            return lax.all_gather(block, "fsdp", axis=0, tiled=False)
        plane = jnp.stack([block] + [self.hop(block, k) for k in (4, 8, 12)])
        pair = jnp.stack([plane, self.hop(plane, 2)], axis=1)
        full = jnp.stack([pair, self.hop(pair, 1)], axis=2)
        full = full.reshape((16,) + block.shape)
        return self.unmix(full)

    def unmix(self, blocks):
        for bit in range(4):
            shape = (8 >> bit, 2, 1 << bit) + blocks.shape[1:]
            turned = blocks.reshape(shape)[:, ::-1].reshape(blocks.shape)
            blocks = jnp.where(jnp.bitwise_and(self.place, 1 << bit) != 0, turned, blocks)
        return blocks

    def scatter_sum(self, blocks):
        if not self.direct:
            return lax.psum_scatter(blocks, "fsdp", scatter_dimension=0, tiled=False).astype(F32)
        core, row, deep = (self.place & 1, (self.place >> 1) & 1, self.place >> 2)
        kind = blocks.dtype
        rest = blocks.shape[1:]

        def pick(value, index, axis):
            return lax.dynamic_index_in_dim(value, index, axis, keepdims=False)

        pairs = blocks.reshape((8, 2) + rest)
        got = self.hop(pick(pairs, 1 - core, 1), 1)
        summed = (pick(pairs, core, 1).astype(F32) + got.astype(F32)).astype(kind)
        pairs = summed.reshape((4, 2) + rest)
        give, keep = pick(pairs, 1 - row, 1), pick(pairs, row, 1)
        total = None
        for k in (3, 2, 1, 0):
            where = jnp.bitwise_xor(deep, k)
            got = self.hop(pick(give, where, 0), 2)
            part = pick(keep, where, 0).astype(F32) + got.astype(F32)
            if k:
                part = self.hop(part.astype(kind), 4 * k).astype(F32)
            total = part if total is None else total + part
        return total

    def scatter_small(self, blocks):
        if not self.direct:
            total = lax.psum_scatter(blocks, "fsdp", scatter_dimension=0, tiled=False)
            return total + self.swap(total)
        mixed = self.unmix(blocks).reshape((4, 2, 2) + blocks.shape[1:])
        mixed = mixed[:, :, 0] + self.hop(mixed[:, :, 1], 1)
        mixed = mixed[:, 0] + self.hop(mixed[:, 1], 2)
        total = mixed[0]
        for k in (1, 2, 3):
            total = total + self.hop(mixed[k], 4 * k)
        return total + self.swap(total)

    def exchange_small(self, blocks):
        mixed = self.unmix(blocks) if self.direct else blocks
        got = lax.all_to_all(mixed, "fsdp", 0, 0, tiled=True)
        return self.unmix(got) if self.direct else got

    def exchange(self, blocks):
        if not self.direct:
            sizes = [g.shape[0] for g in blocks]
            got = lax.all_to_all(jnp.concatenate(blocks), "fsdp", 0, 0, tiled=True)
            out, at = [], 0
            for size in sizes:
                out.append(got[at : at + size])
                at += size
            return out
        out, k = [], 0
        for group in blocks:
            parts = []
            for i in range(group.shape[0]):
                parts.append(self.hop(group[i], k) if k else group[i])
                k += 1
            out.append(jnp.stack(parts))
        return out


def per_device(
    activations,
    cotangent,
    segment_ids,
    routes,
    w_query,
    key_matrix,
    value_matrix,
    w_out,
    w_router,
    gain_attn,
    gain_moe,
    gain_query,
    gain_key,
    w_gate,
    w_up,
    w_down,
):
    ring = Ring()
    half = activations.shape[0]
    tp_count = ring.tp
    devices = ring.size
    rows = half * tp_count
    place_tp = lax.axis_index("tp")
    width = activations.shape[1]
    experts = devices * w_gate.shape[0]
    capacity = rows * routes.shape[1] // experts
    cap = capacity // tp_count
    slots_all = experts * cap
    d_local = w_query.shape[0]
    hidden_half = w_gate.shape[2]
    n_q, n_k = w_query.shape[1], key_matrix.shape[1]
    head = gain_query.shape[0] * devices
    heads, groups = n_q // head, n_k // head
    per_group = heads // groups
    score_scale = head ** (-0.5)

    q_share = gain_query.shape[0]
    line = jnp.concatenate(
        [gain_query, gain_key, jnp.zeros((LANES - 2 * q_share,), BF16)]
    )
    pad_to = max(LANES, d_local)

    def as_line(v):
        return jnp.pad(v, (0, pad_to - v.shape[0]))[None]

    small = jnp.concatenate(
        [
            as_line(gain_attn),
            as_line(gain_moe),
            as_line(line),
            jnp.zeros((5, pad_to), BF16),
            jnp.pad(w_router.T, ((0, 0), (0, pad_to - d_local))),
        ]
    )
    smalls = ring.gather_small(small)
    gain_one = smalls[:, 0, :d_local].reshape(1, width).astype(F32)
    gain_two = smalls[:, 1, :d_local].reshape(1, width).astype(F32)
    gain_q = smalls[:, 2, :q_share].reshape(head).astype(F32)
    gain_k = smalls[:, 2, q_share : 2 * q_share].reshape(head).astype(F32)
    router_t = smalls[:, 8:, :d_local].transpose(1, 0, 2).reshape(experts, width)

    qkv_local = jnp.concatenate([w_query, key_matrix, value_matrix], axis=1)
    qkv_blocks, qkv_last = ring.gather(qkv_local)
    qkv_full = qkv_blocks.reshape(width, n_q + 2 * n_k)
    out_blocks, out_last = ring.gather(after(w_out.T, qkv_last))
    out_full_t = out_blocks.reshape(width, n_q)

    def roll_rows(v):
        return jnp.where(place_tp == 0, v, jnp.roll(v, half, axis=0))

    index = roll_rows(jnp.arange(rows, dtype=jnp.int32))
    segment_row = segment_ids[0]
    segment_rel = roll_rows(segment_row)
    routes_rel = roll_rows(routes)
    first = jnp.min(
        jnp.where(segment_rel[:, None] == segment_rel[None, :], index[None, :], rows), axis=1
    )
    position = (index - first).astype(F32)
    freqs = ROPE_BASE ** (-(2.0 * jnp.arange(head // 2, dtype=F32)) / head)
    angle = position[:, None] * freqs[None, :]
    angle = jnp.concatenate([angle, angle], axis=-1)
    cosine, sine = jnp.cos(angle), jnp.sin(angle)
    allowed = (segment_rel[:, None] == segment_rel[None, :]) & (index[None, :] <= index[:, None])

    def with_other(own):
        return jnp.concatenate([own, ring.swap(own)], axis=0)

    def sum_tp(part, kind):
        return part[:half] + ring.swap(part[half:].astype(kind)).astype(F32)

    expert_ids = jnp.arange(experts, dtype=jnp.int32)
    chosen = jnp.any(routes_rel[:, :, None] == expert_ids[None, None, :], axis=1)
    earlier = (index[None, :] < index[:, None]).astype(BF16)
    before = mm("st,te->se", earlier, chosen.astype(BF16))
    column = jnp.arange(slots_all, dtype=jnp.int32)
    column_expert = ring.order(column // cap)
    spread = (expert_ids[:, None] == column_expert[None, :]).astype(BF16)
    slot_code = jnp.where(chosen, before, -1.0).astype(BF16)
    slot_of = mm("se,ec->sc", slot_code, spread)
    wanted = (column % cap + place_tp * cap).astype(F32)
    dispatch = (slot_of == wanted[None, :]).astype(BF16)

    n_groups = 4 if devices % 4 == 0 else 1
    per = devices // n_groups

    def to_slots(token_rows):
        out = []
        for i in range(n_groups):
            part = dispatch[:, i * per * cap : (i + 1) * per * cap]
            out.append(mm("sc,sd->cd", part, token_rows, BF16).reshape(per, cap, width))
        return out

    gate_own, up_own, down_own = w_gate[0], w_up[0], w_down[0]
    swap_dep = qkv_last
    gate_w = jnp.concatenate([gate_own, ring.swap(after(gate_own, swap_dep))], axis=1)
    up_w = jnp.concatenate([up_own, ring.swap(after(up_own, swap_dep))], axis=1)
    down_w = jnp.concatenate([down_own, ring.swap(after(down_own, swap_dep))], axis=0)

    cot_all = with_other(cotangent)
    cot_groups = ring.exchange(to_slots(after(cot_all, out_last)))
    cot_rows = jnp.concatenate(cot_groups).reshape(slots_all, width)
    grad_hidden = mm("cd,hd->ch", cot_rows, down_w)

    inputs_local = activations.astype(F32)
    scale_one = lax.rsqrt(jnp.mean(inputs_local * inputs_local, axis=-1, keepdims=True) + EPS)
    attention_local = (inputs_local * scale_one * gain_one).astype(BF16)
    attention_input = with_other(attention_local)
    qkv = mm("sd,dc->sc", attention_input, qkv_full)
    query_pre = qkv[:, :n_q].reshape(rows, heads, head)
    key_pre = qkv[:, n_q : n_q + n_k].reshape(rows, groups, head)
    value_bf = qkv[:, n_q + n_k :].astype(BF16).reshape(rows, groups, head)

    def head_norm(v, gain):
        scale = lax.rsqrt(jnp.mean(v * v, axis=-1, keepdims=True) + EPS)
        normed = v * scale * gain
        turned = normed * cosine[:, None, :] + half_turn(normed) * sine[:, None, :]
        return turned.astype(BF16), scale

    query_rot, query_scale = head_norm(query_pre, gain_q)
    key_rot, key_scale = head_norm(key_pre, gain_k)
    query_group = query_rot.reshape(rows, groups, per_group, head)
    scores = mm("iagd,jad->agij", query_group, key_rot) * score_scale
    scores = jnp.where(allowed, scores, -1e30)
    peak = jnp.max(scores, axis=-1, keepdims=True)
    exp_scores = jnp.exp(scores - peak)
    probs = exp_scores / jnp.sum(exp_scores, axis=-1, keepdims=True)
    probs_bf = probs.astype(BF16)
    attended = mm("agij,jad->iagd", probs_bf, value_bf, BF16).reshape(rows, n_q)
    attn_part = mm("sc,dc->sd", attended, out_full_t)
    middle = inputs_local + sum_tp(attn_part, BF16)
    scale_two = lax.rsqrt(jnp.mean(middle * middle, axis=-1, keepdims=True) + EPS)
    moe_local = (middle * scale_two * gain_two).astype(BF16)

    logits = mm("sd,ed->se", moe_local, router_t)
    chosen_local = chosen[:half]
    masked = jnp.where(chosen_local, logits, -jnp.inf)
    top = jnp.max(masked, axis=-1, keepdims=True)
    raised = jnp.exp(masked - top)
    route_weight = raised / jnp.sum(raised, axis=-1, keepdims=True)
    moe_in = with_other(moe_local)
    weight_all = with_other(route_weight.astype(BF16))
    weighted = dispatch * mm("se,ec->sc", weight_all, spread, BF16)

    row_groups = ring.exchange(to_slots(moe_in))
    slot_weight = mm("sc,sl->cl", weighted, jnp.ones((rows, LANES), BF16), BF16)
    weight_recv = ring.exchange_small(slot_weight.reshape(devices, cap, LANES))
    slot_rows = per * cap
    hidden_list, gate_grad_list, up_grad_list, choice_groups, gw_list = [], [], [], [], []
    for i in range(n_groups):
        got = row_groups[i].reshape(slot_rows, width)
        gate_pre = mm("cd,dh->ch", got, gate_w)
        up_pre = mm("cd,dh->ch", got, up_w)
        grad_h = grad_hidden[i * slot_rows : (i + 1) * slot_rows]
        sig = jax.nn.sigmoid(gate_pre)
        silu = gate_pre * sig
        hidden = (silu * up_pre).astype(BF16)
        gate_grad = (grad_h * up_pre * sig * (1.0 + gate_pre * (1.0 - sig))).astype(BF16)
        up_grad = (grad_h * silu).astype(BF16)
        choice = mm("ch,dh->cd", gate_grad, gate_w) + mm("ch,dh->cd", up_grad, up_w)
        choice_groups.append(choice.astype(BF16).reshape(per, cap, width))
        gw = jnp.sum(hidden.astype(F32) * grad_h, axis=-1, keepdims=True)
        gw_list.append(jnp.broadcast_to(gw, (slot_rows, LANES)).astype(BF16))
        hidden_list.append(hidden)
        gate_grad_list.append(gate_grad)
        up_grad_list.append(up_grad)
    gw_recv = ring.exchange_small(jnp.concatenate(gw_list).reshape(devices, cap, LANES))
    choice_back = ring.exchange(choice_groups)
    choice_rows = jnp.concatenate(choice_back).reshape(slots_all, width)

    result_groups = []
    for i in range(n_groups):
        held = after(hidden_list[i], choice_back[-1])
        result_groups.append(mm("ch,hd->cd", held, down_w, BF16).reshape(per, cap, width))
    returned = jnp.concatenate(ring.exchange(result_groups)).reshape(slots_all, width)
    moe_part = mm("sc,cd->sd", weighted, returned)
    block_out = (middle + sum_tp(moe_part, BF16)).astype(BF16)

    weight_col = weight_recv.reshape(slots_all, LANES)[:, :1].astype(F32)
    x_rows = jnp.concatenate(row_groups).reshape(slots_all, width)

    def scaled(parts):
        return (jnp.concatenate(parts).astype(F32) * weight_col).astype(BF16)

    gate_grad_w, up_grad_w, hidden_w = scaled(gate_grad_list), scaled(up_grad_list), scaled(hidden_list)

    def weight_grad(left, right, axis):
        eq = "cd,ch->dh" if axis == 1 else "ch,cd->hd"
        if axis == 1:
            other = mm(eq, left, right[:, hidden_half:], BF16)
            own = mm(eq, left, right[:, :hidden_half])
        else:
            other = mm(eq, left[:, hidden_half:], right, BF16)
            own = mm(eq, left[:, :hidden_half], right)
        return (own + ring.swap(other).astype(F32))[None]

    grad_gate = weight_grad(x_rows, gate_grad_w, 1)
    grad_up = weight_grad(x_rows, up_grad_w, 1)
    grad_down = weight_grad(hidden_w, cot_rows, 0)

    grad_moe_part = mm("sc,cd->sd", weighted, choice_rows)
    lane = jnp.arange(LANES, dtype=jnp.int32)
    spread_back = (column_expert[:, None] == lane[None, :]).astype(BF16)
    gw_cols = gw_recv.reshape(slots_all, LANES) * spread_back
    gw_tokens = mm("sc,cl->sl", dispatch, gw_cols)
    grad_weight = sum_tp(gw_tokens, F32)[:, :experts]
    inner = jnp.sum(route_weight * grad_weight, axis=-1, keepdims=True)
    grad_logits = route_weight * (grad_weight - inner)
    router_float = router_t.astype(F32)
    grad_moe_in = sum_tp(grad_moe_part, BF16) + jnp.dot(grad_logits, router_float, precision=HIGH)
    grad_router_t = jnp.einsum("se,sd->ed", grad_logits, moe_local.astype(F32), precision=HIGH)
    grad_mid_norm, gain_two_rows = norm_back(grad_moe_in, middle, scale_two, gain_two)
    grad_mid = cotangent.astype(F32) + grad_mid_norm
    gain_two_part = jnp.sum(gain_two_rows, axis=0)
    grad_attn_out = with_other(grad_mid.astype(BF16))

    grad_out_part = mm("sd,sc->dc", grad_attn_out, attended, BF16).reshape(devices, d_local, n_q)
    grad_out = ring.scatter_sum(grad_out_part).T
    grad_attended = mm("sd,dc->sc", grad_attn_out, out_full_t, BF16)
    grad_att_group = grad_attended.reshape(rows, groups, per_group, head)
    grad_probs = mm("iagd,jad->agij", grad_att_group, value_bf)
    inner_sum = jnp.sum(probs * grad_probs, axis=-1, keepdims=True)
    grad_scores = (probs * (grad_probs - inner_sum)).astype(BF16)
    grad_value_bf = mm("agij,iagd->jad", probs_bf, grad_att_group, BF16).reshape(rows, n_k)
    grad_query_rot = mm("agij,jad->iagd", grad_scores, key_rot) * score_scale
    grad_query_rot = grad_query_rot.reshape(rows, heads, head)
    grad_key_rot = mm("agij,iagd->jad", grad_scores, query_group) * score_scale

    def turn_back(v):
        return v * cosine[:, None, :] + half_turn_back(v * sine[:, None, :])

    grad_query_raw, gain_q_rows = norm_back(turn_back(grad_query_rot), query_pre, query_scale, gain_q)
    grad_key_raw, gain_k_rows = norm_back(turn_back(grad_key_rot), key_pre, key_scale, gain_k)
    gain_q_part = jnp.sum(gain_q_rows, axis=(0, 1))
    gain_k_part = jnp.sum(gain_k_rows, axis=(0, 1))
    grad_qkv = jnp.concatenate(
        [
            grad_query_raw.reshape(rows, n_q).astype(BF16),
            grad_key_raw.reshape(rows, n_k).astype(BF16),
            grad_value_bf,
        ],
        axis=1,
    )
    grad_qkv_part = mm("sd,sc->dc", attention_input, grad_qkv, BF16)
    grad_qkv_sum = ring.scatter_sum(grad_qkv_part.reshape(devices, d_local, n_q + 2 * n_k))
    grad_attn_in = mm("sc,dc->sd", grad_qkv, qkv_full)
    grad_attn_local = sum_tp(grad_attn_in, F32)
    grad_input_norm, gain_one_rows = norm_back(grad_attn_local, inputs_local, scale_one, gain_one)
    grad_input = (grad_mid + grad_input_norm).astype(BF16)
    gain_one_part = jnp.sum(gain_one_rows, axis=0)

    def lines(v):
        return jnp.pad(v.reshape(devices, 1, -1), ((0, 0), (0, 0), (0, pad_to - v.size // devices)))

    qk_line = jnp.concatenate(
        [gain_q_part.reshape(devices, 1, q_share), gain_k_part.reshape(devices, 1, q_share)], axis=2
    )
    packed = jnp.concatenate(
        [
            lines(gain_one_part),
            lines(gain_two_part),
            jnp.pad(qk_line, ((0, 0), (0, 0), (0, pad_to - 2 * q_share))),
            jnp.zeros((devices, 5, pad_to), F32),
            jnp.pad(
                grad_router_t.reshape(experts, devices, d_local).transpose(1, 0, 2),
                ((0, 0), (0, 0), (0, pad_to - d_local)),
            ),
        ],
        axis=1,
    )
    sums = ring.scatter_small(packed)

    def own_part(v, size):
        return lax.dynamic_slice_in_dim(v, place_tp * (size // tp_count), size // tp_count, 0)

    return (
        block_out,
        grad_input,
        grad_qkv_sum[:, :n_q],
        grad_qkv_sum[:, n_q : n_q + n_k],
        grad_qkv_sum[:, n_q + n_k :],
        grad_out,
        own_part(sums[8:, :d_local].T, d_local),
        own_part(sums[0, :d_local], d_local),
        own_part(sums[1, :d_local], d_local),
        own_part(sums[2, :q_share], q_share),
        own_part(sums[2, q_share : 2 * q_share], q_share),
        grad_gate,
        grad_up,
        grad_down,
    )


def solution(mesh):
    placed = (
        P(("fsdp", "tp"), None),
        P(("fsdp", "tp"), None),
        P("fsdp", None),
        P("fsdp", None),
        P("fsdp", "tp"),
        P("fsdp", "tp"),
        P("fsdp", "tp"),
        P("tp", "fsdp"),
        P("fsdp", None),
        P("fsdp"),
        P("fsdp"),
        P("fsdp"),
        P("fsdp"),
        P("fsdp", None, "tp"),
        P("fsdp", None, "tp"),
        P("fsdp", "tp", None),
    )
    return jax.shard_map(
        per_device,
        mesh=mesh,
        in_specs=placed,
        out_specs=(
            P(("fsdp", "tp"), None),
            P(("fsdp", "tp"), None),
            P("fsdp", "tp"),
            P("fsdp", "tp"),
            P("fsdp", "tp"),
            P("tp", "fsdp"),
            P(("fsdp", "tp"), None),
            P(("fsdp", "tp")),
            P(("fsdp", "tp")),
            P(("fsdp", "tp")),
            P(("fsdp", "tp")),
            P("fsdp", None, "tp"),
            P("fsdp", None, "tp"),
            P("fsdp", "tp", None),
        ),
        check_vma=False,
    )
```
